512 devices in a mesh: seq: 256 (over x, y, z), head: 2 (over core).
Axes of the slice: x: 4, y: 8, z: 8, core: 2. Of those that a mesh axis runs over, the one named last changes fastest.
Arguments:
- queries: bfloat16 [49152, 2560], P('seq', 'head'), may hold values from -6 to 6
- keys: bfloat16 [49152, 2560], P('seq', 'head'), may hold values from -6 to 6
- values: bfloat16 [49152, 2560], P('seq', 'head'), may hold values from -6 to 6
- head_offsets: int32 [5, 20], P(None, 'head'), may hold values from 0 to 15, as said below
- norm_gain: float32 [2560], P('head'), may hold values from 0.1 to 1.9
Outputs:
- attended: bfloat16 [49152, 2560], P('seq', 'head')
- entropy: float32 [20, 49152], P('head', 'seq')
The draws below stay inside these ranges and needn't reach their ends.
Inputs may be any that keep to these rules, and one draw needn't show every extreme that they name: head_offsets[k, h] lies in 0 to 2**k - 1; at each level some head has 2**k - 1.
All inputs are finite; a program needn't handle non-finite values.
Results may differ from the reference program's by a relative error of at most 0.004.
Values may be sent and summed in bfloat16 or wider, within the bound.
A program may use at most 64 MiB of HBM per device.

```python
import math
import jax
import jax.numpy as jnp
from jax import lax

HEADS = 20
DH = 128
D = 2560
TOK_DEV = 192
LEVELS = 5
SEQ = 49152


def draw_queries(key, part):
    result = jnp.clip(jax.random.normal(jax.random.fold_in(key, 1), (SEQ, D), jnp.float32), -6.0, 6.0)
    return result.astype(jnp.bfloat16)


def draw_keys(key, part):
    result = jnp.clip(jax.random.normal(jax.random.fold_in(key, 2), (SEQ, D), jnp.float32), -6.0, 6.0)
    return result.astype(jnp.bfloat16)


def draw_head_offsets(key, part):
    levels_out = []
    for level_index in range(LEVELS):
        dilation = 2 ** level_index
        base = jax.random.randint(jax.random.fold_in(key, 30 + level_index), (HEADS,), 0, dilation)
        marked = jax.random.randint(jax.random.fold_in(key, 60 + level_index), (), 0, HEADS)
        levels_out.append(jnp.where(jnp.arange(HEADS) == marked, dilation - 1, base))
    return jnp.stack(levels_out).astype(jnp.int32)


def block_levels(rng, shape, cuts, low, largest):
    factor_of = 1.0
    for dim, shards_of in cuts:
        heights = jax.random.uniform(jax.random.fold_in(jax.random.fold_in(rng, 6), dim), (shards_of,), jnp.float32, low / len(cuts), largest / len(cuts))
        factor_of = factor_of * jnp.repeat(jnp.exp(heights), shape[dim] // shards_of).reshape((-1,) + (1,) * (len(shape) - 1 - dim))
    return factor_of


def centred(rng, extent, width, most, cuts=(), kind=jnp.bfloat16):
    gain = block_levels(rng, extent, cuts, -0.22, 0.18) if cuts else 1.0
    drawn = jax.random.normal(rng, extent, jnp.float32) * width * gain
    return jnp.minimum(jnp.maximum(drawn, -most), most).astype(kind)


def setup_inputs(seed: int = 0) -> dict:
    arg_keys = jax.random.split(jax.random.key(seed), 6)
    return {
        "queries": draw_queries(jax.random.fold_in(arg_keys[5], 71), 0),
        "keys": draw_keys(jax.random.fold_in(arg_keys[5], 71), 0),
        "values": centred(arg_keys[2], (SEQ, D), 1.0, 6.0, ((0, 256), (1, 2))),
        "head_offsets": draw_head_offsets(jax.random.fold_in(arg_keys[5], 71), 0),
        "norm_gain": jnp.clip(1.0 + 0.18 * jax.random.normal(arg_keys[4], (D,), jnp.float32), 0.1, 1.9),
    }


def select_rows(tensor, chosen, dilation):
    blocks = tensor.reshape(tensor.shape[0] // dilation, dilation, HEADS, DH)
    picked = jnp.einsum('nrhd,hr->nhd', blocks.astype(jnp.float32), chosen.astype(jnp.float32))
    return picked.astype(jnp.bfloat16)

def attend(query_rows, key_rows, value_rows, logit_scale):
    scores = jnp.einsum('qhd,khd->hqk', query_rows.astype(jnp.float32), key_rows.astype(jnp.float32)) * logit_scale
    row_peak = lax.optimization_barrier(jnp.max(scores, axis=2))
    shifted = scores - row_peak[:, :, None]
    weights = jnp.exp(shifted)
    row_total = lax.optimization_barrier(jnp.sum(weights, axis=2))
    spread = lax.optimization_barrier(jnp.sum(weights * shifted, axis=2))
    rounded = lax.optimization_barrier(weights.astype(jnp.bfloat16)).astype(jnp.float32)
    weighted = jnp.einsum('hqk,khd->qhd', rounded, value_rows.astype(jnp.float32))
    return (row_peak, row_total, spread, weighted)

def expand_parts(parts, chosen):
    row_peak, row_total, spread, weighted = parts
    heads, count = row_peak.shape
    dilation = chosen.shape[1]

    def widen(stat):
        return jnp.where(chosen[:, None, :], stat[:, :, None], 0.0).reshape(heads, count * dilation)
    wide_rows = jnp.where(chosen.T[None, :, :, None], weighted[:, None], 0.0).reshape(count * dilation, heads, weighted.shape[2])
    present = jnp.broadcast_to(chosen[:, None, :], (heads, count, dilation)).reshape(heads, count * dilation)
    return ((widen(row_peak), widen(row_total), widen(spread), wide_rows), present)

def merge_level(running, parts, present):
    run_max, run_den, run_spread, run_out = running
    row_peak, row_total, spread, weighted = parts
    row_peak = jnp.where(present, row_peak, run_max)
    new_max = jnp.maximum(run_max, row_peak)
    keep = jnp.exp(run_max - new_max)
    fresh = jnp.where(present, jnp.exp(row_peak - new_max), 0.0)
    denominator = run_den * keep + row_total * fresh
    spread_sum = keep * (run_spread + (run_max - new_max) * run_den) + fresh * (spread + (row_peak - new_max) * row_total)
    output = run_out * keep.T[:, :, None] + weighted * fresh.T[:, :, None]
    return (denominator * 0.0 + new_max, denominator, spread_sum, output)

def one_block(triple, head_offsets):
    block_q, block_k, block_v = triple
    block_len = block_q.shape[0]
    running = None
    for level_index in range(LEVELS):
        dilation = 2 ** level_index
        chosen = jnp.arange(dilation)[None, :] == head_offsets[level_index][:, None]
        query_sel = select_rows(block_q, chosen, dilation)
        key_sel = select_rows(block_k, chosen, dilation)
        value_sel = select_rows(block_v, chosen, dilation)
        segments = block_len // (TOK_DEV * dilation)
        logit_scale = math.log(TOK_DEV * dilation) / math.log(TOK_DEV) / math.sqrt(DH)

        def per_segment(seg_triple):
            return attend(seg_triple[0], seg_triple[1], seg_triple[2], logit_scale)
        shaped = tuple((tensor.reshape(segments, TOK_DEV, HEADS, DH) for tensor in (query_sel, key_sel, value_sel)))
        row_peak, row_total, spread, weighted = lax.map(per_segment, shaped)
        flat_count = segments * TOK_DEV

        def heads_first(stat):
            return stat.transpose(1, 0, 2).reshape(HEADS, flat_count)
        parts = (heads_first(row_peak), heads_first(row_total), heads_first(spread), weighted.reshape(flat_count, HEADS, DH))
        wide, present = expand_parts(parts, chosen)
        if running is None:
            running = wide
        else:
            running = merge_level(running, wide, present)
    run_max, run_den, run_spread, run_out = running
    output = run_out / run_den.T[:, :, None]
    entropy_rows = jnp.log(run_den) - run_spread / run_den
    return (output.reshape(block_len, HEADS * DH), entropy_rows)

def reference(queries, keys, values, head_offsets, norm_gain):
    block_len = 2 ** (LEVELS - 1) * TOK_DEV
    blocks = SEQ // block_len
    shaped = tuple((tensor.reshape(blocks, block_len, HEADS * DH) for tensor in (queries, keys, values)))
    output, entropy_rows = lax.map(lambda triple: one_block(triple, head_offsets), shaped)
    output = output.reshape(SEQ, HEADS * DH)
    entropy = entropy_rows.transpose(1, 0, 2).reshape(HEADS, SEQ)
    mean_square = lax.optimization_barrier(jnp.mean(output * output, axis=1, keepdims=True))
    attended = (output * lax.rsqrt(mean_square + 1e-06) * norm_gain[None, :]).astype(jnp.bfloat16)
    return (attended, entropy)
```

```python
import math

import jax
import jax.numpy as jnp
from jax import lax
from jax.experimental import pallas as pl
from jax.experimental.pallas import tpu as pltpu
from jax.sharding import PartitionSpec as P

DH = 128
TOK = 192
HEADS = 10
LEVELS = 5
MESH = pl.DeviceIdType.MESH
F32 = jnp.float32
BF16 = jnp.bfloat16
SLOTS = {2: 3, 3: 2, 4: 1}
PACK = {2: 144, 3: 80, 4: 48}
BACK = {2: 64, 3: 48, 4: 32}
OUT_ROWS = {2: 48, 3: 32, 4: 16}


def scale_of(level):
    return math.log(TOK * 2**level) / math.log(TOK) / math.sqrt(DH)


def dot(a, b, dims):
    return lax.dot_general(a, b, (dims, ((), ())), preferred_element_type=F32)


def pick(level, offset, rows):
    row = lax.broadcasted_iota(jnp.int32, (rows, TOK), 0)
    token = lax.broadcasted_iota(jnp.int32, (rows, TOK), 1)
    return jnp.where(token == row * 2**level + offset, 1.0, 0.0).astype(F32)


def soft(keys, queries, level):
    scores = dot(keys, queries, ((1,), (1,))) * scale_of(level)
    peak = jnp.max(scores, axis=0, keepdims=True)
    shifted = scores - peak
    weights = jnp.exp(shifted)
    total = jnp.sum(weights, axis=0, keepdims=True)
    spread = jnp.sum(weights * shifted, axis=0, keepdims=True)
    return peak, total, spread, weights.astype(BF16)


def thirds(value):
    high = value.astype(BF16).astype(F32)
    rest = value - high
    middle = rest.astype(BF16).astype(F32)
    return high, middle, rest - middle


def stat_rows(stats):
    width = stats[0].shape[1]
    row = lax.broadcasted_iota(jnp.int32, (16, width), 0)
    result = jnp.zeros((16, width), F32)
    for place, stat in enumerate(stats):
        for part, piece in enumerate(thirds(stat)):
            result = jnp.where(row == 3 * part + place, piece, result)
    return result


def stat_values(rows):
    return tuple(
        rows[6 + i : 7 + i] + rows[3 + i : 4 + i] + rows[i : i + 1] for i in range(3)
    )


def kernel(
    offs, q_ref, k_ref, v_ref, gain_ref, out_ref, ent_ref,
    send1, send2, send3, send4, recv1, recv2, recv3, recv4, query1,
    back2, back3, back4, ret2, ret3, ret4, stats, merged, plain, squares, others,
    s1, s2, s3, s4, r1, r2, r3, r4, t2, t3, t4, u2, u3, u4, sq_sem,
):
    send, recv, back, ret = (
        {2: send2, 3: send3, 4: send4},
        {2: recv2, 3: recv3, 4: recv4},
        {2: back2, 3: back3, 4: back4},
        {2: ret2, 3: ret3, 4: ret4},
    )
    send_sem, recv_sem, back_sem, ret_sem = (
        {2: s2, 3: s3, 4: s4},
        {2: r2, 3: r3, 4: r4},
        {2: t2, 3: t3, 4: t4},
        {2: u2, 3: u3, 4: u4},
    )
    seq = lax.axis_index("seq")
    core = lax.axis_index("head")

    barrier = pltpu.get_barrier_semaphore()
    mine16 = lax.rem(seq, 16)
    for step in range(1, 16):
        peer = seq - mine16 + lax.rem(mine16 + step, 16)
        pl.semaphore_signal(barrier, inc=1, device_id={"seq": peer, "head": core}, device_id_type=MESH)
    pl.semaphore_signal(barrier, inc=1, device_id={"seq": seq, "head": 1 - core}, device_id_type=MESH)

    def columns(h):
        return pl.ds(pl.multiple_of(h * DH, DH), DH)

    @pl.loop(0, HEADS)
    def _(h):
        chosen = jnp.concatenate(
            [pick(1, offs[1, h], 96), pick(2, offs[2, h], 48), pick(3, offs[3, h], 24), pick(4, offs[4, h], 24)],
            axis=0,
        ).astype(BF16)
        keys = dot(chosen, k_ref[:, columns(h)], ((1,), (0,)))
        vals = dot(chosen, v_ref[:, columns(h)], ((1,), (0,)))
        ques = dot(chosen, q_ref[:, columns(h)], ((1,), (0,)))
        send1[h, 0:96] = keys[0:96].astype(BF16)
        send1[h, 96:192] = vals[0:96].astype(BF16)
        query1[h] = ques[0:96].astype(BF16)
        send2[h] = jnp.concatenate([a[96:144] for a in (keys, vals, ques)], axis=0).astype(BF16)
        send3[h] = jnp.concatenate(
            [a[144:168] for a in (keys, vals, ques)] + [jnp.zeros((8, DH), F32)], axis=0
        ).astype(BF16)
        send4[h] = jnp.concatenate([a[168:184] for a in (keys, vals, ques)], axis=0).astype(BF16)

    pl.semaphore_wait(barrier, 16)

    def member(level):
        return lax.rem(seq, 2**level)

    def flip(level, order):
        return order + core * (2**level - 1 - 2 * order)

    def owner(level, h):
        return flip(level, lax.rem(h, 2**level))

    def pack_copy(level, h):
        return pltpu.make_async_remote_copy(
            src_ref=send[level].at[h],
            dst_ref=recv[level].at[h // 2**level, member(level)],
            send_sem=send_sem[level].at[h],
            recv_sem=recv_sem[level].at[h // 2**level, member(level)],
            device_id={"seq": seq - member(level) + owner(level, h), "head": core},
            device_id_type=MESH,
        )

    def near_copy(h):
        return pltpu.make_async_remote_copy(
            src_ref=send1.at[h],
            dst_ref=recv1.at[h],
            send_sem=s1.at[h],
            recv_sem=r1.at[h],
            device_id={"seq": seq + 1 - 2 * lax.rem(seq, 2), "head": core},
            device_id_type=MESH,
        )

    def back_copy(level, slot, m):
        return pltpu.make_async_remote_copy(
            src_ref=back[level].at[slot, m],
            dst_ref=ret[level].at[flip(level, member(level)) + slot * 2**level],
            send_sem=back_sem[level].at[slot, m],
            recv_sem=ret_sem[level].at[flip(level, member(level)) + slot * 2**level],
            device_id={"seq": seq - member(level) + m, "head": core},
            device_id_type=MESH,
        )

    for level in (2, 3, 4):

        @pl.loop(0, HEADS)
        def _(h):
            @pl.when(owner(level, h) != member(level))
            def _():
                pack_copy(level, h).start()

            @pl.when(owner(level, h) == member(level))
            def _():
                recv[level][h // 2**level, member(level)] = send[level][h]

    @pl.loop(0, HEADS)
    def _(h):
        near_copy(h).start()

    @pl.loop(0, HEADS)
    def _(h):
        peak, total, spread, weights = soft(k_ref[:, columns(h)], q_ref[:, columns(h)], 0)
        stats[h, 0:1] = peak
        stats[h, 1:2] = total
        stats[h, 2:3] = spread
        merged[h] = dot(v_ref[:, columns(h)], weights, ((0,), (0,)))

    for level in (2, 3, 4):
        group = 2**level
        rows = TOK // group
        for slot in range(SLOTS[level]):
            held = flip(level, member(level)) + slot * group

            @pl.when(held < HEADS)
            def _():
                for m in range(group):

                    @pl.when(m != member(level))
                    def _():
                        pltpu.make_async_copy(
                            send[level].at[0], recv[level].at[slot, m], recv_sem[level].at[slot, m]
                        ).wait()

                if level == 4:
                    line = lax.broadcasted_iota(jnp.int32, (TOK, 256), 0)
                    place = lax.broadcasted_iota(jnp.int32, (TOK, 256), 1)
                    within = place & 15
                    dense = jnp.where(
                        ((place >> 4) * 12 + within == line) & (within < 12), 1.0, 0.0
                    ).astype(BF16)
                    tall = [
                        jnp.concatenate([recv4[slot, m, 16 * i : 16 * i + 16] for m in range(group)], axis=0)
                        for i in range(3)
                    ]
                    keys = dot(dense, tall[0], ((1,), (0,))).astype(BF16)
                    vals = dot(dense, tall[1], ((1,), (0,))).astype(BF16)
                    ques = tall[2]
                    per = 16
                elif level == 3:
                    wide = [recv3[slot, m].astype(F32) for m in range(group)]
                    keys, vals, ques = (
                        jnp.concatenate([w[rows * i : rows * i + rows] for w in wide], axis=0).astype(BF16)
                        for i in range(3)
                    )
                    per = rows
                else:
                    keys, vals, ques = (
                        jnp.concatenate([recv2[slot, m, rows * i : rows * i + rows] for m in range(group)], axis=0)
                        for i in range(3)
                    )
                    per = rows
                peak, total, spread, weights = soft(keys, ques, level)
                partial = dot(weights, vals, ((0,), (0,)))
                lines = stat_rows((peak, total, spread))
                if lines.shape[1] < 256:
                    lines = jnp.concatenate([lines, jnp.zeros((16, 256 - lines.shape[1]), F32)], axis=1)
                for m in range(group):
                    turned = lines if m == 0 else pltpu.roll(lines, 256 - m * per, 1)
                    pieces = [partial[m * per : m * per + per]]
                    if level == 3:
                        pieces.append(jnp.zeros((8, DH), F32))
                    pieces.append(turned[:, 0:DH])
                    back[level][slot, m] = jnp.concatenate(pieces, axis=0).astype(BF16)
                for m in range(group):

                    @pl.when(m != member(level))
                    def _():
                        back_copy(level, slot, m).start()

                    @pl.when(m == member(level))
                    def _():
                        ret[level][held] = back[level][slot, m]

    def state(h):
        return stats[h, 0:1], stats[h, 1:2], stats[h, 2:3]

    token = lax.broadcasted_iota(jnp.int32, (1, TOK), 1)

    def present(level, h):
        return (token & (2**level - 1)) == offs[level, h]

    @pl.loop(0, HEADS)
    def _(h):
        near_copy(h).wait_recv()
        keys = jnp.concatenate([send1[h, 0:96], recv1[h, 0:96]], axis=0)
        vals = jnp.concatenate([send1[h, 96:192], recv1[h, 96:192]], axis=0)
        peak, total, spread, weights = soft(keys, query1[h], 1)
        partial = dot(vals, weights, ((0,), (0,)))
        high = partial.astype(BF16)
        low = (partial - high.astype(F32)).astype(BF16)
        lines = stat_rows((peak, total, spread)).astype(BF16)
        spots = pick(1, offs[1, h], 96).astype(BF16)
        wide = dot(jnp.concatenate([high, low, lines], axis=0), spots, ((1,), (0,)))
        peak, total, spread = stat_values(wide[2 * DH : 2 * DH + 16])
        there = present(1, h)
        top, mass, moment = state(h)
        peak = jnp.where(there, peak, top)
        new = jnp.maximum(top, peak)
        keep = jnp.exp(top - new)
        fresh = jnp.where(there, jnp.exp(peak - new), 0.0)
        stats[h, 0:1] = new
        stats[h, 1:2] = mass * keep + total * fresh
        stats[h, 2:3] = keep * (moment + (top - new) * mass) + fresh * (spread + (peak - new) * total)
        merged[h] = merged[h] * keep + (wide[0:DH] + wide[DH : 2 * DH]) * fresh

    squares[...] = jnp.zeros_like(squares)

    @pl.loop(0, HEADS)
    def _(h):
        for level in (2, 3, 4):

            @pl.when(owner(level, h) != member(level))
            def _():
                pltpu.make_async_copy(back[level].at[0, 0], ret[level].at[h], ret_sem[level].at[h]).wait()

        top, mass, moment = state(h)
        new = top
        found = []
        for level in (2, 3, 4):
            count = OUT_ROWS[level]
            spots = pick(level, offs[level, h], DH).astype(BF16)
            lines = dot(ret[level][h, count : count + 16], spots, ((1,), (0,)))
            peak, total, spread = stat_values(lines)
            there = present(level, h)
            peak = jnp.where(there, peak, top)
            new = jnp.maximum(new, peak)
            part = dot(ret[level][h, 0:count], spots[0:count], ((0,), (0,)))
            found.append((there, peak, total, spread, part))
        keep = jnp.exp(top - new)
        weight = mass * keep
        sway = keep * (moment + (top - new) * mass)
        factors = []
        for there, peak, total, spread, part in found:
            fresh = jnp.where(there, jnp.exp(peak - new), 0.0)
            weight = weight + total * fresh
            sway = sway + fresh * (spread + (peak - new) * total)
            factors.append(fresh)
        ent_ref[pl.ds(h, 1), :] = jnp.log(weight) - sway / weight
        output = merged[h] * keep
        for (there, peak, total, spread, part), fresh in zip(found, factors):
            output = output + part * fresh
        output = output * (1.0 / weight)
        squares[0:1] += jnp.sum(output * output, axis=0, keepdims=True)
        plain[:, columns(h)] = jnp.transpose(output)

    swap = pltpu.make_async_remote_copy(
        src_ref=squares,
        dst_ref=others,
        send_sem=sq_sem.at[0],
        recv_sem=sq_sem.at[1],
        device_id={"seq": seq, "head": 1 - core},
        device_id_type=MESH,
    )
    swap.start()

    @pl.loop(0, HEADS)
    def _(h):
        near_copy(h).wait_send()
        for level in (2, 3, 4):

            @pl.when(owner(level, h) != member(level))
            def _():
                pack_copy(level, h).wait_send()

    for level in (2, 3, 4):
        for slot in range(SLOTS[level]):

            @pl.when(flip(level, member(level)) + slot * 2**level < HEADS)
            def _():
                for m in range(2**level):

                    @pl.when(m != member(level))
                    def _():
                        back_copy(level, slot, m).wait_send()

    swap.wait()
    square = (squares[0:1] + others[0:1]) / (2 * HEADS * DH)
    factor = lax.rsqrt(square + 1e-06)
    factor = jnp.transpose(jnp.broadcast_to(factor, (DH, TOK)))

    @pl.loop(0, HEADS)
    def _(h):
        out_ref[:, columns(h)] = (plain[:, columns(h)] * factor * gain_ref[:, columns(h)]).astype(BF16)


def shards(queries, keys, values, head_offsets, norm_gain):
    vmem = pl.BlockSpec(memory_space=pltpu.VMEM)
    smem = pl.BlockSpec(memory_space=pltpu.SMEM)
    dma = pltpu.SemaphoreType.DMA

    def buffers(shape_of):
        return [pltpu.VMEM(shape_of(level), BF16) for level in (2, 3, 4)]

    scratch = [pltpu.VMEM((HEADS, TOK, DH), BF16)]
    scratch += buffers(lambda k: (HEADS, PACK[k], DH))
    scratch += [pltpu.VMEM((HEADS, TOK, DH), BF16)]
    scratch += buffers(lambda k: (SLOTS[k], 2**k, PACK[k], DH))
    scratch += [pltpu.VMEM((HEADS, TOK // 2, DH), BF16)]
    scratch += buffers(lambda k: (SLOTS[k], 2**k, BACK[k], DH))
    scratch += buffers(lambda k: (HEADS, BACK[k], DH))
    scratch += [
        pltpu.VMEM((HEADS, 8, TOK), F32),
        pltpu.VMEM((HEADS, DH, TOK), F32),
        pltpu.VMEM((TOK, HEADS * DH), F32),
        pltpu.VMEM((8, TOK), F32),
        pltpu.VMEM((8, TOK), F32),
    ]
    scratch += [dma((HEADS,)) for _ in range(5)]
    scratch += [dma((SLOTS[k], 2**k)) for k in (2, 3, 4)]
    scratch += [dma((SLOTS[k], 2**k)) for k in (2, 3, 4)]
    scratch += [dma((HEADS,)) for _ in range(3)]
    scratch += [dma((2,))]
    return pl.pallas_call(
        kernel,
        out_shape=(
            jax.ShapeDtypeStruct((TOK, HEADS * DH), BF16),
            jax.ShapeDtypeStruct((HEADS, TOK), F32),
        ),
        in_specs=[smem, vmem, vmem, vmem, vmem],
        out_specs=(vmem, vmem),
        scratch_shapes=scratch,
        compiler_params=pltpu.CompilerParams(collective_id=0, has_side_effects=True),
        name="dilated",
    )(head_offsets, queries, keys, values, norm_gain.reshape(1, HEADS * DH))


def solution(mesh):
    in_specs = (P("seq", "head"), P("seq", "head"), P("seq", "head"), P(None, "head"), P("head"))
    out_specs = (P("seq", "head"), P("head", "seq"))
    return jax.shard_map(shards, mesh=mesh, in_specs=in_specs, out_specs=out_specs, check_vma=False)
```

```python
import math

import jax
import jax.numpy as jnp
from jax import lax
from jax.experimental import pallas as pl
from jax.experimental.pallas import tpu as pltpu
from jax.sharding import PartitionSpec as P

DH = 128
TOK = 192
HEADS = 10
LEVELS = 5
MESH = pl.DeviceIdType.MESH
F32 = jnp.float32
BF16 = jnp.bfloat16
SLOTS = {2: 3, 3: 2, 4: 1}
PACK = {2: 144, 3: 80, 4: 48}
BACK = {2: 64, 3: 32, 4: 16}
OUT_ROWS = {2: 48, 3: 32, 4: 16}


def scale_of(level):
    return math.log(TOK * 2**level) / math.log(TOK) / math.sqrt(DH)


def dot(a, b, dims):
    return lax.dot_general(a, b, (dims, ((), ())), preferred_element_type=F32)


def pick(level, offset, rows):
    row = lax.broadcasted_iota(jnp.int32, (rows, TOK), 0)
    token = lax.broadcasted_iota(jnp.int32, (rows, TOK), 1)
    return jnp.where(token == row * 2**level + offset, 1.0, 0.0).astype(F32)


def soft(keys, queries, level):
    scores = dot(keys, queries, ((1,), (1,))) * scale_of(level)
    peak = jnp.max(scores, axis=0, keepdims=True)
    shifted = scores - peak
    weights = jnp.exp(shifted)
    total = jnp.sum(weights, axis=0, keepdims=True)
    spread = jnp.sum(weights * shifted, axis=0, keepdims=True)
    return peak, total, spread, weights.astype(BF16)


def thirds(value):
    high = value.astype(BF16).astype(F32)
    rest = value - high
    middle = rest.astype(BF16).astype(F32)
    return high, middle, rest - middle


def stat_rows(stats):
    width = stats[0].shape[1]
    row = lax.broadcasted_iota(jnp.int32, (16, width), 0)
    result = jnp.zeros((16, width), F32)
    for place, stat in enumerate(stats):
        for part, piece in enumerate(thirds(stat)):
            result = jnp.where(row == 3 * part + place, piece, result)
    return result


def stat_values(rows):
    return tuple(
        rows[6 + i : 7 + i] + rows[3 + i : 4 + i] + rows[i : i + 1] for i in range(3)
    )


def packed_lanes(level):
    count = TOK // 2**level
    lane = lax.broadcasted_iota(jnp.int32, (16, DH), 1).astype(F32)
    return jnp.floor((lane + 0.5) * (1.0 / count))


def pack_stats(lines, level, stride):
    count = TOK // 2**level
    wide = lines.shape[1]
    lane = lax.broadcasted_iota(jnp.int32, (16, wide), 1).astype(F32)
    row = lax.broadcasted_iota(jnp.int32, (16, wide), 0).astype(F32)
    mine = jnp.floor((lane + 0.5) * (1.0 / stride)) == row
    spread = jnp.concatenate([jnp.where(mine, lines[r : r + 1], 0.0) for r in range(9)], axis=0)
    source = lax.broadcasted_iota(jnp.int32, (wide, DH), 0).astype(F32)
    target = lax.broadcasted_iota(jnp.int32, (wide, DH), 1).astype(F32)
    source = source - stride * jnp.floor((source + 0.5) * (1.0 / stride))
    fold = jnp.where((source == target) & (target < count), 1.0, 0.0).astype(BF16)
    moved = dot(spread.astype(BF16), fold, ((1,), (0,)))
    room = DH // count
    results = []
    for first in range(0, 9, room):
        total = moved[16 * first : 16 * first + 16]
        for r in range(first + 1, min(first + room, 9)):
            total = total + pltpu.roll(moved[16 * r : 16 * r + 16], count * (r - first), 1)
        results.append(total)
    return results


def kernel(
    offs, q_ref, k_ref, v_ref, plain, weight_ref, sway_ref, factor_ref,
    send1, send2, send3, send4, recv1, recv2, recv3, recv4, query1,
    back2, back3, back4, ret2, ret3, ret4, stats, merged, squares, others,
    s1, s2, s3, s4, r1, r2, r3, r4, t2, t3, t4, u2, u3, u4, sq_sem,
):
    send, recv, back, ret = (
        {2: send2, 3: send3, 4: send4},
        {2: recv2, 3: recv3, 4: recv4},
        {2: back2, 3: back3, 4: back4},
        {2: ret2, 3: ret3, 4: ret4},
    )
    send_sem, recv_sem, back_sem, ret_sem = (
        {2: s2, 3: s3, 4: s4},
        {2: r2, 3: r3, 4: r4},
        {2: t2, 3: t3, 4: t4},
        {2: u2, 3: u3, 4: u4},
    )
    seq = lax.axis_index("seq")
    core = lax.axis_index("head")

    barrier = pltpu.get_barrier_semaphore()
    mine16 = lax.rem(seq, 16)
    for step in range(1, 16):
        peer = seq - mine16 + lax.rem(mine16 + step, 16)
        pl.semaphore_signal(barrier, inc=1, device_id={"seq": peer, "head": core}, device_id_type=MESH)
    pl.semaphore_signal(barrier, inc=1, device_id={"seq": seq, "head": 1 - core}, device_id_type=MESH)

    def columns(h):
        return pl.ds(pl.multiple_of(h * DH, DH), DH)

    def pack(h):
        chosen = jnp.concatenate(
            [pick(1, offs[1, h], 96), pick(2, offs[2, h], 48), pick(3, offs[3, h], 24), pick(4, offs[4, h], 24)],
            axis=0,
        ).astype(BF16)
        keys = dot(chosen, k_ref[:, columns(h)], ((1,), (0,)))
        vals = dot(chosen, v_ref[:, columns(h)], ((1,), (0,)))
        ques = dot(chosen, q_ref[:, columns(h)], ((1,), (0,)))
        send1[h, 0:96] = keys[0:96].astype(BF16)
        send1[h, 96:192] = vals[0:96].astype(BF16)
        query1[h] = ques[0:96].astype(BF16)
        send2[h] = jnp.concatenate([a[96:144] for a in (keys, vals, ques)], axis=0).astype(BF16)
        send3[h] = jnp.concatenate(
            [a[144:168] for a in (keys, vals, ques)] + [jnp.zeros((8, DH), F32)], axis=0
        ).astype(BF16)
        send4[h] = jnp.concatenate([a[168:184] for a in (keys, vals, ques)], axis=0).astype(BF16)

    def member(level):
        return lax.rem(seq, 2**level)

    def flip(level, order):
        return order + core * (2**level - 1 - 2 * order)

    def owner(level, h):
        return flip(level, lax.rem(h, 2**level))

    def pack_copy(level, h):
        return pltpu.make_async_remote_copy(
            src_ref=send[level].at[h],
            dst_ref=recv[level].at[h // 2**level, member(level)],
            send_sem=send_sem[level].at[h],
            recv_sem=recv_sem[level].at[h // 2**level, member(level)],
            device_id={"seq": seq - member(level) + owner(level, h), "head": core},
            device_id_type=MESH,
        )

    def near_copy(h):
        return pltpu.make_async_remote_copy(
            src_ref=send1.at[h],
            dst_ref=recv1.at[h],
            send_sem=s1.at[h],
            recv_sem=r1.at[h],
            device_id={"seq": seq + 1 - 2 * lax.rem(seq, 2), "head": core},
            device_id_type=MESH,
        )

    def back_copy(level, slot, m):
        return pltpu.make_async_remote_copy(
            src_ref=back[level].at[slot, m],
            dst_ref=ret[level].at[flip(level, member(level)) + slot * 2**level],
            send_sem=back_sem[level].at[slot, m],
            recv_sem=ret_sem[level].at[flip(level, member(level)) + slot * 2**level],
            device_id={"seq": seq - member(level) + m, "head": core},
            device_id_type=MESH,
        )

    @pl.loop(0, HEADS, unroll=5)
    def _(h):
        pack(h)

    pl.semaphore_wait(barrier, 16)

    for level in (4, 3, 2):

        @pl.loop(0, HEADS)
        def _(h):
            @pl.when(owner(level, h) != member(level))
            def _():
                pack_copy(level, h).start()

            @pl.when(owner(level, h) == member(level))
            def _():
                recv[level][h // 2**level, member(level)] = send[level][h]

    @pl.loop(0, HEADS, unroll=5)
    def _(h):
        peak, total, spread, weights = soft(k_ref[:, columns(h)], q_ref[:, columns(h)], 0)
        stats[h, 0:1] = peak
        stats[h, 1:2] = total
        stats[h, 2:3] = spread
        merged[h] = dot(v_ref[:, columns(h)], weights, ((0,), (0,)))

    for level in (4, 3, 2):
        group = 2**level
        rows = TOK // group
        for slot in range(SLOTS[level]):
            held = flip(level, member(level)) + slot * group

            @pl.when(held < HEADS)
            def _():
                for m in range(group):

                    @pl.when(m != member(level))
                    def _():
                        pltpu.make_async_copy(
                            send[level].at[0], recv[level].at[slot, m], recv_sem[level].at[slot, m]
                        ).wait()

                if level == 4:
                    line = lax.broadcasted_iota(jnp.int32, (TOK, 256), 0)
                    place = lax.broadcasted_iota(jnp.int32, (TOK, 256), 1)
                    within = place & 15
                    dense = jnp.where(
                        ((place >> 4) * 12 + within == line) & (within < 12), 1.0, 0.0
                    ).astype(BF16)
                    tall = [
                        jnp.concatenate([recv4[slot, m, 16 * i : 16 * i + 16] for m in range(group)], axis=0)
                        for i in range(3)
                    ]
                    keys = dot(dense, tall[0], ((1,), (0,))).astype(BF16)
                    vals = dot(dense, tall[1], ((1,), (0,))).astype(BF16)
                    ques = tall[2]
                    per = 16
                elif level == 3:
                    wide = [recv3[slot, m].astype(F32) for m in range(group)]
                    keys, vals, ques = (
                        jnp.concatenate([w[rows * i : rows * i + rows] for w in wide], axis=0).astype(BF16)
                        for i in range(3)
                    )
                    per = rows
                else:
                    keys, vals, ques = (
                        jnp.concatenate([recv2[slot, m, rows * i : rows * i + rows] for m in range(group)], axis=0)
                        for i in range(3)
                    )
                    per = rows
                peak, total, spread, weights = soft(keys, ques, level)
                partial = dot(weights, vals, ((0,), (0,)))
                lines = stat_rows((peak, total, spread))
                if level > 2:
                    packed = pack_stats(lines, level, per)
                else:
                    lines = jnp.concatenate([lines, jnp.zeros((16, 256 - TOK), F32)], axis=1)
                for m in range(group):
                    chunk = partial[m * per : m * per + per]
                    if level == 2:
                        turned = lines if m == 0 else pltpu.roll(lines, 256 - m * per, 1)
                        chunk = jnp.concatenate([chunk, turned[:, 0:DH]], axis=0)
                    if level == 3:
                        line = lax.broadcasted_iota(jnp.int32, (8, DH), 0)
                        tail = jnp.where(line == 0, packed[0][m : m + 1], packed[1][m : m + 1])
                        chunk = jnp.concatenate([chunk, tail], axis=0)
                    if level == 4:
                        line = lax.broadcasted_iota(jnp.int32, (16, DH), 0)
                        chunk = jnp.where(line == rows, packed[0][m : m + 1], chunk)
                    back[level][slot, m] = chunk.astype(BF16)
                for m in range(group):

                    @pl.when(m != member(level))
                    def _():
                        back_copy(level, slot, m).start()

                    @pl.when(m == member(level))
                    def _():
                        ret[level][held] = back[level][slot, m]

    @pl.loop(0, HEADS, unroll=5)
    def _(h):
        near_copy(h).start()

    def state(h):
        return stats[h, 0:1], stats[h, 1:2], stats[h, 2:3]

    token = lax.broadcasted_iota(jnp.int32, (1, TOK), 1)

    def present(level, h):
        return (token & (2**level - 1)) == offs[level, h]

    stat_row = lax.broadcasted_iota(jnp.int32, (16, DH), 0).astype(F32)

    def read_lines(level, h):
        count = TOK // 2**level
        spots = pick(level, offs[level, h], OUT_ROWS[level]).astype(BF16)
        if level == 2:
            every = pick(level, offs[level, h], DH).astype(BF16)
            return dot(ret2[h, 48:64], every, ((1,), (0,))), spots
        held = ret[level][h].astype(F32)
        kind = packed_lanes(level)
        room = DH // count
        lines = jnp.where(kind == stat_row, held[count : count + 1], 0.0)
        if room < 9:
            lines = jnp.where((kind < room) & (stat_row < room), lines, 0.0)
            lines = lines + jnp.where((kind < room) & (kind + room == stat_row), held[count + 1 : count + 2], 0.0)
        lane = lax.broadcasted_iota(jnp.int32, (DH, TOK), 0).astype(F32)
        token_of = lax.broadcasted_iota(jnp.int32, (DH, TOK), 1)
        query = lane - count * jnp.floor((lane + 0.5) * (1.0 / count))
        every = jnp.where(token_of == query.astype(jnp.int32) * 2**level + offs[level, h], 1.0, 0.0)
        return dot(lines.astype(BF16), every.astype(BF16), ((1,), (0,))), spots

    @pl.loop(0, HEADS, unroll=5)
    def _(h):
        for level in (2, 3, 4):

            @pl.when(owner(level, h) != member(level))
            def _():
                pltpu.make_async_copy(back[level].at[0, 0], ret[level].at[h], ret_sem[level].at[h]).wait()

        top, mass, moment = state(h)
        new = top
        found = []
        for level in (2, 3, 4):
            lines, spots = read_lines(level, h)
            peak, total, spread = stat_values(lines)
            there = present(level, h)
            peak = jnp.where(there, peak, top)
            new = jnp.maximum(new, peak)
            part = dot(ret[level][h, 0 : OUT_ROWS[level]], spots, ((0,), (0,)))
            found.append((there, peak, total, spread, part))
        keep = jnp.exp(top - new)
        weight = mass * keep
        sway = keep * (moment + (top - new) * mass)
        output = merged[h] * keep
        for there, peak, total, spread, part in found:
            fresh = jnp.where(there, jnp.exp(peak - new), 0.0)
            weight = weight + total * fresh
            sway = sway + fresh * (spread + (peak - new) * total)
            output = output + part * fresh
        stats[h, 0:1] = new
        stats[h, 1:2] = weight
        stats[h, 2:3] = sway
        merged[h] = output

    squares[...] = jnp.zeros_like(squares)

    @pl.loop(0, HEADS, unroll=5)
    def _(h):
        near_copy(h).wait_recv()
        keys = jnp.concatenate([send1[h, 0:96], recv1[h, 0:96]], axis=0)
        vals = jnp.concatenate([send1[h, 96:192], recv1[h, 96:192]], axis=0)
        peak, total, spread, weights = soft(keys, query1[h], 1)
        partial = dot(vals, weights, ((0,), (0,)))
        high = partial.astype(BF16)
        low = (partial - high.astype(F32)).astype(BF16)
        lines = stat_rows((peak, total, spread)).astype(BF16)
        spots = pick(1, offs[1, h], 96).astype(BF16)
        wide = dot(jnp.concatenate([high, low, lines], axis=0), spots, ((1,), (0,)))
        peak, total, spread = stat_values(wide[2 * DH : 2 * DH + 16])
        there = present(1, h)
        top, mass, moment = state(h)
        peak = jnp.where(there, peak, top)
        new = jnp.maximum(top, peak)
        keep = jnp.exp(top - new)
        fresh = jnp.where(there, jnp.exp(peak - new), 0.0)
        weight = mass * keep + total * fresh
        weight_ref[pl.ds(h, 1), :] = weight
        sway_ref[pl.ds(h, 1), :] = keep * (moment + (top - new) * mass) + fresh * (spread + (peak - new) * total)
        scale = 1.0 / weight
        output = merged[h] * (keep * scale) + (wide[0:DH] + wide[DH : 2 * DH]) * (fresh * scale)
        squares[0:1] += jnp.sum(output * output, axis=0, keepdims=True)
        plain[:, columns(h)] = jnp.transpose(output)

    swap = pltpu.make_async_remote_copy(
        src_ref=squares,
        dst_ref=others,
        send_sem=sq_sem.at[0],
        recv_sem=sq_sem.at[1],
        device_id={"seq": seq, "head": 1 - core},
        device_id_type=MESH,
    )
    swap.start()

    @pl.loop(0, HEADS, unroll=5)
    def _(h):
        near_copy(h).wait_send()
        for level in (2, 3, 4):

            @pl.when(owner(level, h) != member(level))
            def _():
                pack_copy(level, h).wait_send()

    for level in (2, 3, 4):
        for slot in range(SLOTS[level]):

            @pl.when(flip(level, member(level)) + slot * 2**level < HEADS)
            def _():
                for m in range(2**level):

                    @pl.when(m != member(level))
                    def _():
                        back_copy(level, slot, m).wait_send()

    swap.wait()
    square = (squares[0:1] + others[0:1]) / (2 * HEADS * DH)
    factor = lax.rsqrt(square + 1e-06)
    factor_ref[...] = jnp.transpose(jnp.broadcast_to(factor, (DH, TOK)))


def finish(plain_ref, factor_ref, gain_ref, weight_ref, sway_ref, out_ref, ent_ref):
    factor = factor_ref[...]
    for h in range(HEADS):
        lanes = pl.ds(h * DH, DH)
        gain = gain_ref[lanes].reshape(1, DH)
        out_ref[:, lanes] = (plain_ref[:, lanes] * factor * gain).astype(BF16)
    weight = weight_ref[...]
    ent_ref[...] = jnp.log(weight) - sway_ref[...] / weight


def shards(queries, keys, values, head_offsets, norm_gain):
    vmem = pl.BlockSpec(memory_space=pltpu.VMEM)
    smem = pl.BlockSpec(memory_space=pltpu.SMEM)
    dma = pltpu.SemaphoreType.DMA

    def buffers(shape_of):
        return [pltpu.VMEM(shape_of(level), BF16) for level in (2, 3, 4)]

    scratch = [pltpu.VMEM((HEADS, TOK, DH), BF16)]
    scratch += buffers(lambda k: (HEADS, PACK[k], DH))
    scratch += [pltpu.VMEM((HEADS, TOK, DH), BF16)]
    scratch += buffers(lambda k: (SLOTS[k], 2**k, PACK[k], DH))
    scratch += [pltpu.VMEM((HEADS, TOK // 2, DH), BF16)]
    scratch += buffers(lambda k: (SLOTS[k], 2**k, BACK[k], DH))
    scratch += buffers(lambda k: (HEADS, BACK[k], DH))
    scratch += [
        pltpu.VMEM((HEADS, 8, TOK), F32),
        pltpu.VMEM((HEADS, DH, TOK), F32),
        pltpu.VMEM((8, TOK), F32),
        pltpu.VMEM((8, TOK), F32),
    ]
    scratch += [dma((HEADS,)) for _ in range(5)]
    scratch += [dma((SLOTS[k], 2**k)) for k in (2, 3, 4)]
    scratch += [dma((SLOTS[k], 2**k)) for k in (2, 3, 4)]
    scratch += [dma((HEADS,)) for _ in range(3)]
    scratch += [dma((2,))]
    plain, weight, sway, factor = pl.pallas_call(
        kernel,
        out_shape=(
            jax.ShapeDtypeStruct((TOK, HEADS * DH), F32),
            jax.ShapeDtypeStruct((HEADS, TOK), F32),
            jax.ShapeDtypeStruct((HEADS, TOK), F32),
            jax.ShapeDtypeStruct((TOK, DH), F32),
        ),
        in_specs=[smem, vmem, vmem, vmem],
        out_specs=(vmem, vmem, vmem, vmem),
        scratch_shapes=scratch,
        compiler_params=pltpu.CompilerParams(collective_id=0, has_side_effects=True),
        name="dilated",
    )(head_offsets, queries, keys, values)
    return pl.pallas_call(
        finish,
        out_shape=(
            jax.ShapeDtypeStruct((TOK, HEADS * DH), BF16),
            jax.ShapeDtypeStruct((HEADS, TOK), F32),
        ),
        in_specs=[vmem] * 5,
        out_specs=(vmem, vmem),
        name="finish",
    )(plain, factor, norm_gain, weight, sway)


def solution(mesh):
    in_specs = (P("seq", "head"), P("seq", "head"), P("seq", "head"), P(None, "head"), P("head"))
    out_specs = (P("seq", "head"), P("head", "seq"))
    return jax.shard_map(shards, mesh=mesh, in_specs=in_specs, out_specs=out_specs, check_vma=False)
```

```python
import math

import jax
import jax.numpy as jnp
from jax import lax
from jax.experimental import pallas as pl
from jax.experimental.pallas import tpu as pltpu
from jax.sharding import PartitionSpec as P

DH = 128
TOK = 192
HEADS = 10
LEVELS = 5
FINISH = 640
MESH = pl.DeviceIdType.MESH
F32 = jnp.float32
BF16 = jnp.bfloat16
SLOTS = {2: 3, 3: 2, 4: 1}
PACK = {2: 144, 3: 80, 4: 48}
SENT = {2: 144, 3: 72, 4: 48}
BACK = {2: 64, 3: 32, 4: 16}
OUT_ROWS = {2: 48, 3: 32, 4: 16}


def scale_of(level):
    return math.log(TOK * 2**level) / math.log(TOK) / math.sqrt(DH)


def dot(a, b, dims):
    return lax.dot_general(a, b, (dims, ((), ())), preferred_element_type=F32)


def pick(level, offset, rows):
    row = lax.broadcasted_iota(jnp.int32, (rows, TOK), 0)
    token = lax.broadcasted_iota(jnp.int32, (rows, TOK), 1)
    return jnp.where(token == row * 2**level + offset, 1.0, 0.0).astype(F32)


def soft(keys, queries, level):
    scores = dot(keys, queries, ((1,), (1,))) * scale_of(level)
    peak = jnp.max(scores, axis=0, keepdims=True)
    shifted = scores - peak
    weights = jnp.exp(shifted)
    total = jnp.sum(weights, axis=0, keepdims=True)
    spread = jnp.sum(weights * shifted, axis=0, keepdims=True)
    return peak, total, spread, weights.astype(BF16)


def thirds(value):
    high = value.astype(BF16).astype(F32)
    rest = value - high
    middle = rest.astype(BF16).astype(F32)
    return high, middle, rest - middle


def stat_rows(stats):
    width = stats[0].shape[1]
    row = lax.broadcasted_iota(jnp.int32, (16, width), 0)
    result = jnp.zeros((16, width), F32)
    for place, stat in enumerate(stats):
        for part, piece in enumerate(thirds(stat)):
            result = jnp.where(row == 3 * part + place, piece, result)
    return result


def stat_values(rows):
    return tuple(
        rows[6 + i : 7 + i] + rows[3 + i : 4 + i] + rows[i : i + 1] for i in range(3)
    )


def packed_lanes(level):
    count = TOK // 2**level
    lane = lax.broadcasted_iota(jnp.int32, (16, DH), 1).astype(F32)
    return jnp.floor((lane + 0.5) * (1.0 / count))


def pack_stats(lines, level, stride):
    count = TOK // 2**level
    wide = lines.shape[1]
    lane = lax.broadcasted_iota(jnp.int32, (16, wide), 1).astype(F32)
    row = lax.broadcasted_iota(jnp.int32, (16, wide), 0).astype(F32)
    mine = jnp.floor((lane + 0.5) * (1.0 / stride)) == row
    spread = jnp.concatenate([jnp.where(mine, lines[r : r + 1], 0.0) for r in range(9)], axis=0)
    source = lax.broadcasted_iota(jnp.int32, (wide, DH), 0).astype(F32)
    target = lax.broadcasted_iota(jnp.int32, (wide, DH), 1).astype(F32)
    source = source - stride * jnp.floor((source + 0.5) * (1.0 / stride))
    fold = jnp.where((source == target) & (target < count), 1.0, 0.0).astype(BF16)
    moved = dot(spread.astype(BF16), fold, ((1,), (0,)))
    room = DH // count
    results = []
    for first in range(0, 9, room):
        total = moved[16 * first : 16 * first + 16]
        for r in range(first + 1, min(first + room, 9)):
            total = total + pltpu.roll(moved[16 * r : 16 * r + 16], count * (r - first), 1)
        results.append(total)
    return results


def kernel(
    offs, q_ref, k_ref, v_ref, plain, weight_ref, sway_ref, factor_ref,
    send1, send2, send3, send4, recv1, recv2, recv3, recv4, query1,
    back2, back3, back4, ret2, ret3, ret4, stats, merged, squares, others,
    s1, s2, s3, s4, r1, r2, r3, r4, t2, t3, t4, u2, u3, u4, sq_sem,
):
    send, recv, back, ret = (
        {2: send2, 3: send3, 4: send4},
        {2: recv2, 3: recv3, 4: recv4},
        {2: back2, 3: back3, 4: back4},
        {2: ret2, 3: ret3, 4: ret4},
    )
    send_sem, recv_sem, back_sem, ret_sem = (
        {2: s2, 3: s3, 4: s4},
        {2: r2, 3: r3, 4: r4},
        {2: t2, 3: t3, 4: t4},
        {2: u2, 3: u3, 4: u4},
    )
    seq = lax.axis_index("seq")
    core = lax.axis_index("head")

    barrier = pltpu.get_barrier_semaphore()
    mine16 = lax.rem(seq, 16)
    for step in range(1, 16):
        peer = seq - mine16 + lax.rem(mine16 + step, 16)
        pl.semaphore_signal(barrier, inc=1, device_id={"seq": peer, "head": core}, device_id_type=MESH)
    pl.semaphore_signal(barrier, inc=1, device_id={"seq": seq, "head": 1 - core}, device_id_type=MESH)

    def columns(h):
        return pl.ds(pl.multiple_of(h * DH, DH), DH)

    def pack(h):
        chosen = jnp.concatenate(
            [pick(1, offs[1, h], 96), pick(2, offs[2, h], 48), pick(3, offs[3, h], 24), pick(4, offs[4, h], 24)],
            axis=0,
        ).astype(BF16)
        keys = dot(chosen, k_ref[:, columns(h)], ((1,), (0,)))
        vals = dot(chosen, v_ref[:, columns(h)], ((1,), (0,)))
        ques = dot(chosen, q_ref[:, columns(h)], ((1,), (0,)))
        send1[h, 0:96] = keys[0:96].astype(BF16)
        send1[h, 96:192] = vals[0:96].astype(BF16)
        query1[h] = ques[0:96].astype(BF16)
        send2[h] = jnp.concatenate([a[96:144] for a in (keys, vals, ques)], axis=0).astype(BF16)
        send3[h] = jnp.concatenate(
            [a[144:168] for a in (keys, vals, ques)] + [jnp.zeros((8, DH), F32)], axis=0
        ).astype(BF16)
        send4[h] = jnp.concatenate([a[168:184] for a in (keys, vals, ques)], axis=0).astype(BF16)

    def member(level):
        return lax.rem(seq, 2**level)

    def flip(level, order):
        return order + core * (2**level - 1 - 2 * order)

    def owner(level, h):
        return flip(level, lax.rem(h, 2**level))

    def pack_copy(level, h):
        return pltpu.make_async_remote_copy(
            src_ref=send[level].at[h, pl.ds(0, SENT[level])],
            dst_ref=recv[level].at[h // 2**level, member(level), pl.ds(0, SENT[level])],
            send_sem=send_sem[level].at[h],
            recv_sem=recv_sem[level].at[h // 2**level, member(level)],
            device_id={"seq": seq - member(level) + owner(level, h), "head": core},
            device_id_type=MESH,
        )

    def near_copy(h):
        return pltpu.make_async_remote_copy(
            src_ref=send1.at[h],
            dst_ref=recv1.at[h],
            send_sem=s1.at[h],
            recv_sem=r1.at[h],
            device_id={"seq": seq + 1 - 2 * lax.rem(seq, 2), "head": core},
            device_id_type=MESH,
        )

    def back_copy(level, slot, m):
        return pltpu.make_async_remote_copy(
            src_ref=back[level].at[slot, m],
            dst_ref=ret[level].at[flip(level, member(level)) + slot * 2**level],
            send_sem=back_sem[level].at[slot, m],
            recv_sem=ret_sem[level].at[flip(level, member(level)) + slot * 2**level],
            device_id={"seq": seq - member(level) + m, "head": core},
            device_id_type=MESH,
        )

    def send_packs(level, first, last):
        @pl.loop(first, last)
        def _(h):
            @pl.when(owner(level, h) != member(level))
            def _():
                pack_copy(level, h).start()

            @pl.when(owner(level, h) == member(level))
            def _():
                recv[level][h // 2**level, member(level)] = send[level][h]

    half = HEADS // 2

    @pl.loop(0, half, unroll=5)
    def _(h):
        pack(h)

    pl.semaphore_wait(barrier, 16)
    send_packs(4, 0, half)
    send_packs(3, 0, half)

    @pl.loop(half, HEADS, unroll=5)
    def _(h):
        pack(h)

    send_packs(4, half, HEADS)
    send_packs(3, half, HEADS)
    send_packs(2, 0, HEADS)

    @pl.loop(0, HEADS, unroll=5)
    def _(h):
        peak, total, spread, weights = soft(k_ref[:, columns(h)], q_ref[:, columns(h)], 0)
        stats[h, 0:1] = peak
        stats[h, 1:2] = total
        stats[h, 2:3] = spread
        merged[h] = dot(v_ref[:, columns(h)], weights, ((0,), (0,)))

    for level in (4, 3, 2):
        group = 2**level
        rows = TOK // group
        for slot in range(SLOTS[level]):
            held = flip(level, member(level)) + slot * group

            @pl.when(held < HEADS)
            def _():
                for m in range(group):

                    @pl.when(m != member(level))
                    def _():
                        pltpu.make_async_copy(
                            send[level].at[0, pl.ds(0, SENT[level])], recv[level].at[slot, m, pl.ds(0, SENT[level])], recv_sem[level].at[slot, m]
                        ).wait()

                if level == 4:
                    line = lax.broadcasted_iota(jnp.int32, (TOK, 256), 0)
                    place = lax.broadcasted_iota(jnp.int32, (TOK, 256), 1)
                    within = place & 15
                    dense = jnp.where(
                        ((place >> 4) * 12 + within == line) & (within < 12), 1.0, 0.0
                    ).astype(BF16)
                    tall = [
                        jnp.concatenate([recv4[slot, m, 16 * i : 16 * i + 16] for m in range(group)], axis=0)
                        for i in range(3)
                    ]
                    keys = dot(dense, tall[0], ((1,), (0,))).astype(BF16)
                    vals = dot(dense, tall[1], ((1,), (0,))).astype(BF16)
                    ques = tall[2]
                    per = 16
                elif level == 3:
                    wide = [recv3[slot, m].astype(F32) for m in range(group)]
                    keys, vals, ques = (
                        jnp.concatenate([w[rows * i : rows * i + rows] for w in wide], axis=0).astype(BF16)
                        for i in range(3)
                    )
                    per = rows
                else:
                    keys, vals, ques = (
                        jnp.concatenate([recv2[slot, m, rows * i : rows * i + rows] for m in range(group)], axis=0)
                        for i in range(3)
                    )
                    per = rows
                peak, total, spread, weights = soft(keys, ques, level)
                partial = dot(weights, vals, ((0,), (0,)))
                lines = stat_rows((peak, total, spread))
                if level > 2:
                    packed = pack_stats(lines, level, per)
                else:
                    lines = jnp.concatenate([lines, jnp.zeros((16, 256 - TOK), F32)], axis=1)
                for m in range(group):
                    chunk = partial[m * per : m * per + per]
                    if level == 2:
                        turned = lines if m == 0 else pltpu.roll(lines, 256 - m * per, 1)
                        chunk = jnp.concatenate([chunk, turned[:, 0:DH]], axis=0)
                    if level == 3:
                        line = lax.broadcasted_iota(jnp.int32, (8, DH), 0)
                        tail = jnp.where(line == 0, packed[0][m : m + 1], packed[1][m : m + 1])
                        chunk = jnp.concatenate([chunk, tail], axis=0)
                    if level == 4:
                        line = lax.broadcasted_iota(jnp.int32, (16, DH), 0)
                        chunk = jnp.where(line == rows, packed[0][m : m + 1], chunk)
                    back[level][slot, m] = chunk.astype(BF16)
                for m in range(group):

                    @pl.when(m != member(level))
                    def _():
                        back_copy(level, slot, m).start()

                    @pl.when(m == member(level))
                    def _():
                        ret[level][held] = back[level][slot, m]

    @pl.loop(0, HEADS, unroll=5)
    def _(h):
        near_copy(h).start()

    def state(h):
        return stats[h, 0:1], stats[h, 1:2], stats[h, 2:3]

    token = lax.broadcasted_iota(jnp.int32, (1, TOK), 1)

    def present(level, h):
        return (token & (2**level - 1)) == offs[level, h]

    stat_row = lax.broadcasted_iota(jnp.int32, (16, DH), 0).astype(F32)

    def read_lines(level, h):
        count = TOK // 2**level
        spots = pick(level, offs[level, h], OUT_ROWS[level]).astype(BF16)
        if level == 2:
            every = pick(level, offs[level, h], DH).astype(BF16)
            return dot(ret2[h, 48:64], every, ((1,), (0,))), spots
        held = ret[level][h].astype(F32)
        kind = packed_lanes(level)
        room = DH // count
        lines = jnp.where(kind == stat_row, held[count : count + 1], 0.0)
        if room < 9:
            lines = jnp.where((kind < room) & (stat_row < room), lines, 0.0)
            lines = lines + jnp.where((kind < room) & (kind + room == stat_row), held[count + 1 : count + 2], 0.0)
        lane = lax.broadcasted_iota(jnp.int32, (DH, TOK), 0).astype(F32)
        token_of = lax.broadcasted_iota(jnp.int32, (DH, TOK), 1)
        query = lane - count * jnp.floor((lane + 0.5) * (1.0 / count))
        every = jnp.where(token_of == query.astype(jnp.int32) * 2**level + offs[level, h], 1.0, 0.0)
        return dot(lines.astype(BF16), every.astype(BF16), ((1,), (0,))), spots

    @pl.loop(0, HEADS, unroll=5)
    def _(h):
        for level in (2, 3, 4):

            @pl.when(owner(level, h) != member(level))
            def _():
                pltpu.make_async_copy(back[level].at[0, 0], ret[level].at[h], ret_sem[level].at[h]).wait()

        top, mass, moment = state(h)
        new = top
        found = []
        for level in (2, 3, 4):
            lines, spots = read_lines(level, h)
            peak, total, spread = stat_values(lines)
            there = present(level, h)
            peak = jnp.where(there, peak, top)
            new = jnp.maximum(new, peak)
            part = dot(ret[level][h, 0 : OUT_ROWS[level]], spots, ((0,), (0,)))
            found.append((there, peak, total, spread, part))
        keep = jnp.exp(top - new)
        weight = mass * keep
        sway = keep * (moment + (top - new) * mass)
        output = merged[h] * keep
        for there, peak, total, spread, part in found:
            fresh = jnp.where(there, jnp.exp(peak - new), 0.0)
            weight = weight + total * fresh
            sway = sway + fresh * (spread + (peak - new) * total)
            output = output + part * fresh
        stats[h, 0:1] = new
        stats[h, 1:2] = weight
        stats[h, 2:3] = sway
        merged[h] = output

    squares[...] = jnp.zeros_like(squares)

    @pl.loop(0, HEADS, unroll=5)
    def _(h):
        near_copy(h).wait_recv()
        keys = jnp.concatenate([send1[h, 0:96], recv1[h, 0:96]], axis=0)
        vals = jnp.concatenate([send1[h, 96:192], recv1[h, 96:192]], axis=0)
        peak, total, spread, weights = soft(keys, query1[h], 1)
        partial = dot(vals, weights, ((0,), (0,)))
        high = partial.astype(BF16)
        low = (partial - high.astype(F32)).astype(BF16)
        lines = stat_rows((peak, total, spread)).astype(BF16)
        spots = pick(1, offs[1, h], 96).astype(BF16)
        wide = dot(jnp.concatenate([high, low, lines], axis=0), spots, ((1,), (0,)))
        peak, total, spread = stat_values(wide[2 * DH : 2 * DH + 16])
        there = present(1, h)
        top, mass, moment = state(h)
        peak = jnp.where(there, peak, top)
        new = jnp.maximum(top, peak)
        keep = jnp.exp(top - new)
        fresh = jnp.where(there, jnp.exp(peak - new), 0.0)
        weight = mass * keep + total * fresh
        weight_ref[pl.ds(h, 1), :] = weight
        sway_ref[pl.ds(h, 1), :] = keep * (moment + (top - new) * mass) + fresh * (spread + (peak - new) * total)
        scale = 1.0 / weight
        output = merged[h] * (keep * scale) + (wide[0:DH] + wide[DH : 2 * DH]) * (fresh * scale)
        squares[0:1] += jnp.sum(output * output, axis=0, keepdims=True)
        plain[:, columns(h)] = jnp.transpose(output)

    swap = pltpu.make_async_remote_copy(
        src_ref=squares,
        dst_ref=others,
        send_sem=sq_sem.at[0],
        recv_sem=sq_sem.at[1],
        device_id={"seq": seq, "head": 1 - core},
        device_id_type=MESH,
    )
    swap.start()

    @pl.loop(0, HEADS, unroll=5)
    def _(h):
        near_copy(h).wait_send()
        for level in (2, 3, 4):

            @pl.when(owner(level, h) != member(level))
            def _():
                pack_copy(level, h).wait_send()

    for level in (2, 3, 4):
        for slot in range(SLOTS[level]):

            @pl.when(flip(level, member(level)) + slot * 2**level < HEADS)
            def _():
                for m in range(2**level):

                    @pl.when(m != member(level))
                    def _():
                        back_copy(level, slot, m).wait_send()

    swap.wait()
    square = (squares[0:1] + others[0:1]) / (2 * HEADS * DH)
    factor = lax.rsqrt(square + 1e-06)
    factor_ref[...] = jnp.transpose(jnp.broadcast_to(factor, (DH, TOK)))


def finish(plain_ref, factor_ref, gain_ref, weight_ref, sway_ref, out_ref, ent_ref):
    factor = factor_ref[...]
    for h in range(FINISH // DH):
        lanes = pl.ds(h * DH, DH)
        gain = gain_ref[pl.ds(pl.multiple_of(pl.program_id(0) * FINISH + h * DH, DH), DH)].reshape(1, DH)
        out_ref[:, lanes] = (plain_ref[:, lanes] * factor * gain).astype(BF16)

    @pl.when(pl.program_id(0) == 0)
    def _():
        weight = weight_ref[...]
        ent_ref[...] = jnp.log(weight) - sway_ref[...] / weight


def shards(queries, keys, values, head_offsets, norm_gain):
    vmem = pl.BlockSpec(memory_space=pltpu.VMEM)
    smem = pl.BlockSpec(memory_space=pltpu.SMEM)
    dma = pltpu.SemaphoreType.DMA

    def buffers(shape_of):
        return [pltpu.VMEM(shape_of(level), BF16) for level in (2, 3, 4)]

    scratch = [pltpu.VMEM((HEADS, TOK, DH), BF16)]
    scratch += buffers(lambda k: (HEADS, PACK[k], DH))
    scratch += [pltpu.VMEM((HEADS, TOK, DH), BF16)]
    scratch += buffers(lambda k: (SLOTS[k], 2**k, PACK[k], DH))
    scratch += [pltpu.VMEM((HEADS, TOK // 2, DH), BF16)]
    scratch += buffers(lambda k: (SLOTS[k], 2**k, BACK[k], DH))
    scratch += buffers(lambda k: (HEADS, BACK[k], DH))
    scratch += [
        pltpu.VMEM((HEADS, 8, TOK), F32),
        pltpu.VMEM((HEADS, DH, TOK), F32),
        pltpu.VMEM((8, TOK), F32),
        pltpu.VMEM((8, TOK), F32),
    ]
    scratch += [dma((HEADS,)) for _ in range(5)]
    scratch += [dma((SLOTS[k], 2**k)) for k in (2, 3, 4)]
    scratch += [dma((SLOTS[k], 2**k)) for k in (2, 3, 4)]
    scratch += [dma((HEADS,)) for _ in range(3)]
    scratch += [dma((2,))]
    plain, weight, sway, factor = pl.pallas_call(
        kernel,
        out_shape=(
            jax.ShapeDtypeStruct((TOK, HEADS * DH), F32),
            jax.ShapeDtypeStruct((HEADS, TOK), F32),
            jax.ShapeDtypeStruct((HEADS, TOK), F32),
            jax.ShapeDtypeStruct((TOK, DH), F32),
        ),
        in_specs=[smem, vmem, vmem, vmem],
        out_specs=(vmem, vmem, vmem, vmem),
        scratch_shapes=scratch,
        compiler_params=pltpu.CompilerParams(collective_id=0, has_side_effects=True),
        name="dilated",
    )(head_offsets, queries, keys, values)
    return pl.pallas_call(
        finish,
        out_shape=(
            jax.ShapeDtypeStruct((TOK, HEADS * DH), BF16),
            jax.ShapeDtypeStruct((HEADS, TOK), F32),
        ),
        grid=(HEADS * DH // FINISH,),
        in_specs=[
            pl.BlockSpec((TOK, FINISH), lambda i: (0, i)),
            pl.BlockSpec((TOK, DH), lambda i: (0, 0)),
            vmem,
            pl.BlockSpec((HEADS, TOK), lambda i: (0, 0)),
            pl.BlockSpec((HEADS, TOK), lambda i: (0, 0)),
        ],
        out_specs=(
            pl.BlockSpec((TOK, FINISH), lambda i: (0, i)),
            pl.BlockSpec((HEADS, TOK), lambda i: (0, 0)),
        ),
        name="finish",
    )(plain, factor, norm_gain, weight, sway)


def solution(mesh):
    in_specs = (P("seq", "head"), P("seq", "head"), P("seq", "head"), P(None, "head"), P("head"))
    out_specs = (P("seq", "head"), P("head", "seq"))
    return jax.shard_map(shards, mesh=mesh, in_specs=in_specs, out_specs=out_specs, check_vma=False)
```
